128 devices in a mesh: gx: 4 (over x), gy: 32 (over z, y, core).
Axes of the slice: x: 4, y: 4, z: 4, core: 2. Of those that a mesh axis runs over, the one named last changes fastest.
Arguments:
- particles: bfloat16 [131072, 128], P(('gx', 'gy')), may hold values from -6 to 6
- weights: bfloat16 [131072], P(('gx', 'gy')), may hold values from 0.099609375 to 1
- detections: bfloat16 [65536, 128], P(('gx', 'gy')), may hold values from -6 to 6
- clutter: float32 [65536], P(('gx', 'gy')), may hold values from 4096 to 40960
- gate_ids: int32 [1024, 16], P(('gx', 'gy')), may hold values from 0 to 127, all different within a row; in each aligned block of 8 rows (0 to 7, 8 to 15, ...) at most 2 rows name the same one
- gate_lens: int32 [1024], P(('gx', 'gy')), may hold values from 10 to 16
Outputs:
- updated: float32 [131072], P(('gx', 'gy'))
- log_norm: float32 [65536], P(('gx', 'gy'))
- estimate: float32 [65536, 128], P(('gx', 'gy'))
The draws below stay inside these ranges and needn't reach their ends.
Inputs may be any that keep to these rules, and one draw needn't show every extreme that they name: `gate_ids`: each row names 16 different detection blocks, of which only the first gate_lens entries are used. Over the 8 rows of one device no detection block is named more than 2 times, and some device names some block exactly 2 times.
All inputs are finite; a program needn't handle non-finite values.
Results may differ from the reference program's by a relative error of at most 0.00084.
Values may be sent and summed in bfloat16 or wider, within the bound.
No kernel may reach another device: no remote copies, remote signals or barrier semaphores. Data moves between devices by JAX's collectives and lax.ppermute only.
A program may use at most 64 MiB of HBM per device.

```python
import math
import jax
import jax.numpy as jnp
import numpy as np
from jax import lax

F = 128
PBS = 128
DBS = 512
P_BLK = 8
G_MAX = 16
G_MIN = 10
CAP = 2
DBLOCKS = 128
PBLOCKS = 1024
PARTICLES = 131072
DETS = 65536


def draw_gate_lens(key, part):
    lengths = jax.random.randint(key, (PBLOCKS,), G_MIN, G_MAX + 1, dtype=jnp.int32)
    lengths = lengths.at[0].set(G_MAX)
    lengths = lengths.at[1].set(G_MIN)
    return lengths


def level_of(own_key, extent, cuts, low, top_value):
    def one(dim, parts):
        draws = jax.random.uniform(jax.random.fold_in(jax.random.fold_in(own_key, 6), dim), (parts,), jnp.float32, low / len(cuts), top_value / len(cuts))
        return jnp.repeat(jnp.exp(draws), extent[dim] // parts).reshape((-1,) + (1,) * (len(extent) - dim - 1))

    factor_of = one(*cuts[0])
    for cut in cuts[1:]:
        factor_of = factor_of * one(*cut)
    return factor_of


def routed_block(stream_key, own, number, rows, number_of, top, limit, slope):
    sequence = jax.random.permutation(stream_key, number_of)
    heavy_load, usual = shares(number_of, rows * top, limit, slope, True), shares(number_of, rows * top, limit, slope, False)
    places = jnp.arange(number_of)

    def named(sizes, rotation):
        used = int((sizes > 0).sum())
        fixed = max(1, used // 4)
        passed = fixed + (places - fixed + rotation * (used - fixed)) % max(1, number_of - fixed)
        return jnp.zeros((number_of,), jnp.int32).at[sequence[jnp.where(places < fixed, places, passed)]].set(jnp.asarray(sizes, jnp.int32))

    sizes = jnp.where(number % 4 == 0, named(heavy_load, number // 4), named(usual, number - number // 4 - 1))
    mixed = jax.random.permutation(jax.random.fold_in(own, 3), number_of)
    source_of, receiver = mixed[0:number_of // 2 * 2:2], mixed[1:number_of // 2 * 2:2]
    slack = jnp.minimum(sizes[source_of] - 1, limit - sizes[receiver]) // 2
    slack = jnp.where((source_of == sequence[0]) | (receiver == sequence[0]) | (sizes[receiver] == 0), 0, jnp.maximum(slack, 0))
    passed = jax.random.randint(jax.random.fold_in(own, 4), (number_of // 2,), 0, 1 << 20) % (slack + 1)
    sizes = sizes.at[source_of].add(-passed).at[receiver].add(passed)
    members = jnp.searchsorted(jnp.cumsum(sizes), jnp.arange(rows * top), side="right").astype(jnp.int32)
    table = members.reshape(top, rows).T
    table = table[jax.random.permutation(jax.random.fold_in(own, 1), rows)]
    rotation = jax.random.randint(jax.random.fold_in(own, 2), (rows, 1), 0, top)
    return jnp.take_along_axis(table, (jnp.arange(top)[None, :] + rotation) % top, axis=1)


def shares(count, total, bound, lean, full):
    portions = [(1 << 20) // math.isqrt(standing ** lean) + 1 for standing in range(1, count + 1)]
    largest = bound if full else min(bound, max(-(-total // count), total * portions[0] // sum(portions)))
    least = 1 if total - largest >= count - 1 else 0
    given, rest = [largest] + [least] * (count - 1), total - largest - least * (count - 1)
    while rest > 0:
        movable = [i for i in range(1, count) if given[i] < largest] or [i for i in range(1, count) if given[i] < bound]
        mass, budget = sum([portions[i] for i in movable]), rest
        for i in movable:
            extra = min(bound - given[i], max(1, budget * portions[i] // mass), rest)
            given[i] = given[i] + extra
            rest = rest - extra
    return np.array(given)


def gaussian(rng, extent, deviation, bound, cuts=(), kind=jnp.bfloat16):
    array = deviation * jax.random.normal(rng, extent, jnp.float32)
    if cuts:
        array = array * level_of(rng, extent, cuts, -0.22, 0.18)
    return jnp.clip(array, -bound, bound).astype(kind)


def setup_inputs(seed: int = 0) -> dict:
    splits = jax.random.split(jax.random.key(seed), 7)
    particles = gaussian(splits[0], (PARTICLES, F), 1.0, 6.0, ((0, 128),))
    weights = jnp.clip(jnp.exp(math.log(1.0) - 2.306499 * jax.random.uniform(splits[1], (PARTICLES,), jnp.float32) ** level_of(splits[1], (PARTICLES,), ((0, 128),), -0.2, 0.2)), 0.099609375, 1.0).astype(jnp.bfloat16)
    detections = gaussian(splits[2], (DETS, F), 1.0, 6.0, ((0, 128),))
    clutter = jnp.clip(jnp.exp(math.log(40960.0) - 2.3025851 * jax.random.uniform(splits[3], (DETS,), jnp.float32) ** level_of(splits[3], (DETS,), ((0, 128),), -0.2, 0.2)), 4096.0, 40960.0)
    gate_ids_keys = jax.random.split(jax.random.fold_in(splits[4], 1), PBLOCKS // P_BLK)
    gate_ids_turns = jax.random.permutation(jax.random.fold_in(splits[4], 3), PBLOCKS // P_BLK)
    gate_ids = jax.vmap(lambda own, number: routed_block(jax.random.fold_in(splits[4], 2), own, number, P_BLK, DBLOCKS, G_MAX, CAP, 2))(gate_ids_keys, gate_ids_turns).reshape((PBLOCKS, G_MAX))
    gate_lens = draw_gate_lens(jax.random.fold_in(splits[6], 71), 0)
    return {"particles": particles, "weights": weights, "detections": detections, "clutter": clutter, "gate_ids": gate_ids, "gate_lens": gate_lens}


DETECT_PROB = 0.9
SPREAD = 8.0


def reference(particles, weights, detections, clutter, gate_ids, gate_lens):
    features = particles.shape[1]
    offset = features / 8.0
    det_blocks = detections.reshape(DBLOCKS, DBS, features).astype(jnp.float32)
    det_half = 0.5 * jnp.sum(jnp.square(det_blocks), axis=2)
    part_blocks = particles.reshape(PBLOCKS, PBS, features)
    weight_blocks = weights.astype(jnp.float32).reshape(PBLOCKS, PBS)
    live_mask = (jnp.arange(G_MAX, dtype=jnp.int32)[None, :] < gate_lens[:, None]).astype(jnp.float32)

    def likelihood_tiles(block_rows, block_ids):
        block_float = block_rows.astype(jnp.float32)
        rows_half = 0.5 * jnp.sum(jnp.square(block_float), axis=1)
        cross_term = jnp.einsum("rf,gdf->grd", block_float, det_blocks[block_ids], precision=lax.Precision.HIGHEST)
        return jnp.exp((cross_term - rows_half[None, :, None] - det_half[block_ids][:, None, :]) / SPREAD + offset)

    def first_pass(running, inputs):
        mass_sum, moment = running
        block_rows, block_weights, block_ids, live_rows = inputs
        weighted = likelihood_tiles(block_rows, block_ids) * block_weights[None, :, None] * live_rows[:, None, None]
        mass_sum = mass_sum.at[block_ids].add(jnp.sum(weighted, axis=1))
        weighted_low = weighted.astype(jnp.bfloat16).astype(jnp.float32)
        moment = moment.at[block_ids].add(jnp.einsum("grd,rf->gdf", weighted_low, block_rows.astype(jnp.float32), precision=lax.Precision.HIGHEST))
        return (mass_sum, moment), None

    start_state = (jnp.zeros((DBLOCKS, DBS), jnp.float32), jnp.zeros((DBLOCKS, DBS, features), jnp.float32))
    (mass_sum, moment), unused = lax.scan(first_pass, start_state, (part_blocks, weight_blocks, gate_ids, live_mask))
    normalizer = clutter.reshape(DBLOCKS, DBS) + DETECT_PROB * mass_sum
    log_norm = jnp.log(normalizer)
    estimate = DETECT_PROB * moment / normalizer[:, :, None]
    inverse_low = (1.0 / normalizer).astype(jnp.bfloat16).astype(jnp.float32)

    def second_pass(running, inputs):
        block_rows, block_ids, live_rows = inputs
        likelihood_low = likelihood_tiles(block_rows, block_ids).astype(jnp.bfloat16).astype(jnp.float32)
        partial_value = jnp.einsum("grd,gd->gr", likelihood_low, inverse_low[block_ids], precision=lax.Precision.HIGHEST)
        return running, jnp.sum(partial_value * live_rows[:, None], axis=0)

    unused, share = lax.scan(second_pass, jnp.zeros((), jnp.float32), (part_blocks, gate_ids, live_mask))
    updated = weights.astype(jnp.float32) * ((1.0 - DETECT_PROB) + DETECT_PROB * share.reshape(-1))
    return updated, log_norm.reshape(-1), estimate.reshape(DBLOCKS * DBS, features)
```

```python
import jax
import jax.numpy as jnp
from jax import lax
from jax.experimental import pallas as pl
from jax.experimental.pallas import tpu as pltpu
from jax.sharding import PartitionSpec as P

PBS = 128
DBS = 512
DETECT_PROB = 0.9
LOG2E = 1.4426950408889634
SCALE = LOG2E / 8.0
BLOCKS = 128
SLOTS = 136
META = 1024
ROWS = 1072

f32 = jnp.float32
bf16 = jnp.bfloat16


def alpha_groups():
    return [[a * 2 + c for a in range(16)] for c in range(2)]


def core_swap(v):
    return lax.ppermute(v, "gy", [(i, i ^ 1) for i in range(32)])


def x_shift(v, s):
    return lax.ppermute(v, "gx", [(i, (i + s) % 4) for i in range(4)])


def pair_kernel(mask_ref, pos_ref, recv_ref, det_ref, as_ref, mom_ref, mass_ref, low_ref, slot_ref,
                lst, wrow, brow, buf, sem):
    x, c = pos_ref[0], pos_ref[1]
    for s in range(16):
        wb = recv_ref[s, META:META + 16, :].astype(f32)
        ml = recv_ref[s, META + 16:META + 32, :].astype(f32)
        wrow[s * 8:(s + 1) * 8, :] = wb[:8]
        brow[s * 8:(s + 1) * 8, :] = wb[8:] + ml[:8] + ml[8:]
    wrow[BLOCKS:BLOCKS + 8, :] = jnp.zeros((8, 128), f32)
    mom_ref[...] = jnp.zeros_like(mom_ref)
    mass_ref[...] = jnp.zeros_like(mass_ref)

    bits = [((x + 4 - r // 2) % 4) * 2 + (c ^ (r % 2)) for r in range(8)]

    def scan_block(b, counts):
        m = mask_ref[b]
        out = []
        for r in range(8):
            lst[r, counts[r]] = b
            out.append(counts[r] + ((m >> bits[r]) & 1))
        return tuple(out)

    counts = lax.fori_loop(0, BLOCKS, scan_block, tuple(jnp.int32(0) for _ in range(8)))
    q = jnp.int32(0)
    for r in range(8):
        cnt = counts[r]

        def fill(p, q, r=r, cnt=cnt):
            slot_ref[0, q] = lst[r, 2 * p]
            slot_ref[1, q] = jnp.where(2 * p + 1 < cnt, lst[r, 2 * p + 1], BLOCKS)
            slot_ref[2, q] = r
            return q + 1

        q = lax.fori_loop(0, (cnt + 1) // 2, fill, q)
    slot_ref[3, 0] = q
    n = q

    def copy_out(q, s):
        return pltpu.make_async_copy(buf.at[s], low_ref.at[q], sem.at[s])

    def step(q, carry):
        b0, b1, r = slot_ref[0, q], slot_ref[1, q], slot_ref[2, q]
        b1c = jnp.minimum(b1, BLOCKS - 1)
        x2 = jnp.concatenate(
            [recv_ref[b0 // 8, pl.ds((b0 % 8) * PBS, PBS), :], recv_ref[b1c // 8, pl.ds((b1c % 8) * PBS, PBS), :]],
            axis=0,
        )
        w2 = jnp.concatenate([wrow[pl.ds(b0, 1), :], wrow[pl.ds(b1, 1), :]], axis=1)
        s2 = jnp.concatenate([brow[pl.ds(b0, 1), :], brow[pl.ds(b1c, 1), :]], axis=1)
        slot = q & 1

        @pl.when(q >= 2)
        def _():
            copy_out(q - 2, slot).wait()

        half = DBS // 2
        for h in range(2):
            rows = slice(h * half, (h + 1) * half)
            cross = lax.dot_general(det_ref[r, rows, :], x2, (((1,), (1,)), ((), ())), preferred_element_type=f32)
            a = as_ref[r, rows, :]
            lik = jnp.exp2(cross * SCALE + (jnp.concatenate([a, a], axis=1) + s2))
            buf[slot, rows, :] = lik.astype(bf16)
            wtd = lik * w2
            mass_ref[r, rows, :] += wtd[:, :128] + wtd[:, 128:]
            mom_ref[r, rows, :] += jnp.dot(wtd.astype(bf16), x2, preferred_element_type=f32)
        copy_out(q, slot).start()
        return carry

    lax.fori_loop(0, n, step, 0)

    @pl.when(n >= 2)
    def _():
        copy_out(n - 2, n & 1).wait()

    @pl.when(n >= 1)
    def _():
        copy_out(n - 1, (n - 1) & 1).wait()


def share_kernel(slot_ref, inv_ref, low_ref, share_ref, buf, sem):
    share_ref[...] = jnp.zeros_like(share_ref)
    n = slot_ref[3, 0]
    depth = buf.shape[0]

    def copy_in(q, s):
        return pltpu.make_async_copy(low_ref.at[q], buf.at[s], sem.at[s])

    for d in range(depth):
        @pl.when(d < n)
        def _(d=d):
            copy_in(d, d).start()

    def step(q, carry):
        s = q % depth
        copy_in(q, s).wait()
        b0, b1, r = slot_ref[0, q], slot_ref[1, q], slot_ref[2, q]
        v = inv_ref[r]
        low = buf[s].astype(f32)
        t = jnp.sum(low * jnp.concatenate([v, v], axis=1), axis=0, keepdims=True)
        share_ref[pl.ds(b0, 1), :] += t[:, :128]
        share_ref[pl.ds(b1, 1), :] += t[:, 128:]

        @pl.when(q + depth < n)
        def _():
            copy_in(q + depth, s).start()

        return carry

    lax.fori_loop(0, n, step, 0)


def local(particles, weights, detections, clutter, gate_ids, gate_lens):
    gx, gy = lax.axis_index("gx"), lax.axis_index("gy")
    c, alpha = gy % 2, gy // 2

    two = jnp.stack([detections, core_swap(detections)])
    dets = jnp.concatenate([two] + [x_shift(two, s) for s in (1, 2, 3)])

    half = jnp.sum(jnp.square(particles.astype(f32)), axis=1).reshape(8, PBS) * (-0.5 * SCALE)
    hi = lax.reduce_precision(half, 8, 7)
    mid = lax.reduce_precision(half - hi, 8, 7)
    lo = (half - hi) - mid
    live = jnp.arange(16, dtype=jnp.int32)[None, :] < gate_lens[:, None]
    bit = jnp.where(live, 1 << ((gate_ids // 32) * 2 + gate_ids % 2), 0)
    home = (gate_ids % 32) // 2
    masks = jnp.sum(jnp.where(home[:, :, None] == jnp.arange(16)[None, None, :], bit[:, :, None], 0), axis=1)
    payload = jnp.concatenate(
        [
            particles,
            weights.reshape(8, PBS),
            hi.astype(bf16),
            mid.astype(bf16),
            lo.astype(bf16),
            jnp.pad(masks.astype(bf16).reshape(1, 128), ((0, 15), (0, 0))),
        ]
    )
    recv = lax.all_gather(payload, "gy", axis_index_groups=alpha_groups())
    got = lax.dynamic_index_in_dim(recv[:, META + 32, :].reshape(BLOCKS, 16), alpha, 1, keepdims=False)

    dsq = jnp.sum(jnp.square(dets.astype(f32)), axis=2) * (-0.5 * SCALE) + 16.0 * LOG2E
    as_b = jnp.broadcast_to(dsq[:, :, None], (8, DBS, 128))

    vm = pl.BlockSpec(memory_space=pltpu.VMEM)
    sm = pl.BlockSpec(memory_space=pltpu.SMEM)
    hb = pl.BlockSpec(memory_space=pl.ANY)
    mom, mass, low, slots = pl.pallas_call(
        pair_kernel,
        out_shape=(
            jax.ShapeDtypeStruct((8, DBS, 128), f32),
            jax.ShapeDtypeStruct((8, DBS, 128), f32),
            jax.ShapeDtypeStruct((SLOTS, DBS, 256), bf16),
            jax.ShapeDtypeStruct((4, SLOTS), jnp.int32),
        ),
        in_specs=[sm, sm, vm, vm, vm],
        out_specs=(vm, vm, hb, sm),
        scratch_shapes=[
            pltpu.SMEM((8, BLOCKS + 8), jnp.int32),
            pltpu.VMEM((BLOCKS + 8, 128), f32),
            pltpu.VMEM((BLOCKS, 128), f32),
            pltpu.VMEM((2, DBS, 256), bf16),
            pltpu.SemaphoreType.DMA((2,)),
        ],
        compiler_params=pltpu.CompilerParams(vmem_limit_bytes=40 << 20),
        name="pairs",
    )(got.astype(jnp.int32), jnp.stack([gx, c]).astype(jnp.int32), recv, dets, as_b)

    part = jnp.sum(mass, axis=2) * DETECT_PROB
    part = part + jnp.pad(clutter.reshape(1, DBS), ((0, 7), (0, 0)))
    part = part.reshape(4, 2, DBS)
    other = core_swap(part)
    part = part + other[:, ::-1]
    norm = part
    for s in (1, 2, 3):
        norm = norm + jnp.roll(x_shift(part, s), s, axis=0)
    inv = (1.0 / norm).astype(bf16).astype(f32)
    inv_b = jnp.broadcast_to(inv.reshape(8, DBS)[:, :, None], (8, DBS, 128))

    share = pl.pallas_call(
        share_kernel,
        out_shape=jax.ShapeDtypeStruct((BLOCKS + 8, 128), f32),
        in_specs=[sm, vm, hb],
        out_specs=vm,
        scratch_shapes=[pltpu.VMEM((4, DBS, 256), bf16), pltpu.SemaphoreType.DMA((4,))],
        compiler_params=pltpu.CompilerParams(vmem_limit_bytes=24 << 20),
        name="shares",
    )(slots, inv_b, low)
    back = lax.all_to_all(
        share[:BLOCKS].reshape(16, 8, 128), "gy", split_axis=0, concat_axis=0, axis_index_groups=alpha_groups()
    )
    total = jnp.sum(back, axis=0).reshape(-1)
    updated = weights.astype(f32) * ((1.0 - DETECT_PROB) + DETECT_PROB * total)

    mom = mom.reshape(4, 2, DBS, 128)
    own = mom[:, 0] + core_swap(mom[:, 1])
    moment = own[0]
    for s in (1, 2, 3):
        moment = moment + x_shift(own[s], -s)
    normalizer = norm[0, 0]
    return updated, jnp.log(normalizer), DETECT_PROB * moment / normalizer[:, None]


def solution(mesh):
    both = P(("gx", "gy"))
    rows = P(("gx", "gy"), None)
    return jax.shard_map(
        local,
        mesh=mesh,
        in_specs=(rows, both, rows, both, rows, both),
        out_specs=(both, both, rows),
        check_vma=False,
    )
```

```python
import functools

import jax
import jax.numpy as jnp
from jax import lax
from jax.experimental import pallas as pl
from jax.experimental.pallas import tpu as pltpu
from jax.sharding import PartitionSpec as P

PBS = 128
DBS = 512
DETECT_PROB = 0.9
LOG2E = 1.4426950408889634
SCALE = LOG2E / 8.0
HB = 4
META = HB * PBS
ROWS = META + 32
TABLE = 152
LOW = 76
RING = 8
DUMMY = 8
NONE = 128

f32 = jnp.float32
bf16 = jnp.bfloat16


def alpha_groups():
    return [[a * 2 + c for a in range(16)] for c in range(2)]


def gy_shift(v, dz, dy, dc=0):
    perm = []
    for i in range(32):
        z, y, c = i // 8, i // 2 % 4, i % 2
        perm.append((i, (z + dz) % 4 * 8 + (y + dy) % 4 * 2 + (c + dc) % 2))
    return lax.ppermute(v, "gy", perm)


def x_shift(v, s):
    return lax.ppermute(v, "gx", [(i, (i + s) % 4) for i in range(4)])


def x_swap(v, s):
    return lax.ppermute(v, "gx", [(i, i ^ s) for i in range(4)])


def pair_kernel(steps, before, *refs):
    parts = 2 * len(steps)
    count = parts * 16
    pos_ref, refs = refs[0], refs[1:]
    part_refs, refs = refs[:parts], refs[parts:]
    det_ref, refs = refs[0], refs[1:]
    first = before == 0
    tables, refs = refs[:before], refs[before:]
    if not first:
        as_ref, refs = refs[0], refs[2:]
    mom_ref, mass_ref, low_ref, slot_ref, refs = refs[0], refs[1], refs[2], refs[3], refs[4:]
    if first:
        as_ref, refs = refs[0], refs[1:]
    lst, gates, grow, meta, xs, wrow, brow, cr0, cr1, w0, w1, ring, sem, xsem, msem = refs
    c, z, y = pos_ref[0], pos_ref[1], pos_ref[2]
    lane = (z * 4 + y) * HB

    heads = [
        pltpu.make_async_copy(part_refs[t].at[:, pl.ds(META, 32), :], meta.at[pl.ds(4 * t, 4)], msem.at[t])
        for t in range(parts)
    ]
    loads = [
        pltpu.make_async_copy(part_refs[t].at[:, pl.ds(0, META), :], xs.at[pl.ds(4 * t, 4)], xsem.at[t])
        for t in range(parts)
    ]
    for copy in heads + loads:
        copy.start()
    mom_ref[...] = jnp.zeros_like(mom_ref)
    mass_ref[...] = jnp.zeros_like(mass_ref)
    if first:
        for r in range(8):
            for h in range(0, DBS, 128):
                d = det_ref[r, h:h + 128, :].astype(f32)
                v = jnp.sum(d * d, axis=1, keepdims=True) * (-0.5 * SCALE) + 16.0 * LOG2E
                as_ref[r, h:h + 128, :] = jnp.broadcast_to(v, (128, 128))
    base = jnp.int32(0)
    for table in tables:
        base = base + (table[3, 0] + 1) // 2
    for copy in heads:
        copy.wait()
    for s in range(parts * 4):
        grow[s:s + 1, :] = meta[s, 16:32, :].astype(f32)[0:1].astype(jnp.int32)
    gate_load = pltpu.make_async_copy(grow, gates, msem.at[0])
    gate_load.start()
    for s in range(parts * 4):
        rows = meta[s, 0:16, :].astype(f32)
        wrow[s * 4:(s + 1) * 4, :] = rows[0:4]
        brow[s * 4:(s + 1) * 4, :] = rows[4:8] + rows[8:12] + rows[12:16]
    wrow[count:count + 8, :] = jnp.zeros((8, 128), f32)
    gate_load.wait()

    bits = [r ^ c for r in range(8)]
    counts = [jnp.int32(0)] * 8
    for s in range(parts * 4):
        h, step, u = s // 4 % 2, steps[s // 8], s % 4
        dz, dy = (step, u) if h == 0 else (u, step)
        home = (((z + 4 - dz) % 4) * 4 + (y + 4 - dy) % 4) * 8 + h * 4
        for j in range(HB):
            m = gates[s, lane + j]
            v = (home + j) * 256 + (s * 4 + j)
            for r in range(8):
                lst[r, counts[r]] = v
                counts[r] = counts[r] + ((m >> bits[r]) & 1)

    def put(q, v0, v1, r):
        slot_ref[0, q] = v0
        slot_ref[1, q] = v1
        slot_ref[2, q] = r

    hole = NONE * 256 + count
    put(0, 0, hole, DUMMY)
    q = jnp.int32(1)
    for r in range(8):
        cnt = counts[r]

        def fill(p, q, r=r, cnt=cnt):
            put(q, lst[r, 2 * p], jnp.where(2 * p + 1 < cnt, lst[r, 2 * p + 1], hole), r)
            return q + 1

        q = lax.fori_loop(0, (cnt + 1) // 2, fill, q)
    for d in range(3):
        put(q + d, NONE * 256, hole, DUMMY)
    n = q - 1
    slot_ref[3, 0] = n
    for copy in loads:
        copy.wait()

    cr, w = (cr0, cr1), (w0, w1)

    def copy_out(p, j):
        return pltpu.make_async_copy(ring.at[j], low_ref.at[p], sem.at[j])

    def both(q):
        b0 = slot_ref[0, q] & 255
        b1 = jnp.minimum(slot_ref[1, q] & 255, count - 1)
        return jnp.concatenate(
            [xs[b // 4, pl.ds(pl.multiple_of(b % 4 * PBS, PBS), PBS), :] for b in (b0, b1)], axis=0
        )

    def cross(q, s):
        r = jnp.minimum(slot_ref[2, q], 7)
        cr[s][...] = lax.dot_general(det_ref[r], both(q), (((1,), (1,)), ((), ())), preferred_element_type=f32)

    def likelihood(q, s, j):
        b0, b1, r = slot_ref[0, q] & 255, slot_ref[1, q] & 255, slot_ref[2, q]
        b1c, rc = jnp.minimum(b1, count - 1), jnp.minimum(r, 7)
        w2 = jnp.concatenate([wrow[pl.ds(b0, 1), :], wrow[pl.ds(b1, 1), :]], axis=1)
        s2 = jnp.concatenate([brow[pl.ds(b0, 1), :], brow[pl.ds(b1c, 1), :]], axis=1)
        for h in range(0, DBS, 32):
            rows = slice(h, h + 32)
            a = as_ref[rc, rows, :]
            lik = jnp.exp2(cr[s][rows, :] * SCALE + (jnp.concatenate([a, a], axis=1) + s2))
            ring[j, 1 - s, rows, :] = lik.astype(bf16)
            wtd = lik * w2
            mass_ref[r, rows, :] += wtd[:, :128] + wtd[:, 128:]
            w[s][rows, :] = wtd.astype(bf16)

    def moment(q, s):
        r = slot_ref[2, q]
        mom_ref[jnp.where(r < DUMMY, r // 2 + r % 2 * 4, DUMMY)] += jnp.dot(w[s][...], both(q), preferred_element_type=f32)

    cross(1, 1)

    def body(p, carry):
        q = 2 * p + 2
        j = lax.rem(p, RING)

        @pl.when(p >= RING)
        def _():
            copy_out(0, j).wait()

        cross(q, 0)
        likelihood(q - 1, 1, j)
        moment(q - 2, 0)
        cross(q + 1, 1)
        likelihood(q, 0, j)
        moment(q - 1, 1)
        copy_out(base + p, j).start()
        return carry

    total = (n + 2) // 2
    lax.fori_loop(0, total, body, 0)

    def drain(j, carry):
        copy_out(0, j).wait()
        return carry

    lax.fori_loop(0, jnp.minimum(total, RING), drain, 0)


def pair_call(steps, pos, parts, dets, tables, state):
    n = len(parts)
    first = state is None
    vm = pl.BlockSpec(memory_space=pltpu.VMEM)
    sm = pl.BlockSpec(memory_space=pltpu.SMEM)
    hb = pl.BlockSpec(memory_space=pl.ANY)
    acc = jax.ShapeDtypeStruct((9, DBS, 128), f32)
    low = jax.ShapeDtypeStruct((LOW, 2, DBS, 256), bf16)
    table = jax.ShapeDtypeStruct((4, TABLE), jnp.int32)
    operands, specs = [pos] + parts + [dets], [sm] + [hb] * n + [vm]
    outs, out_specs = [acc, acc, low, table], [vm, vm, hb, sm]
    aliases = {}
    if first:
        outs, out_specs = outs + [jax.ShapeDtypeStruct((8, DBS, 128), f32)], out_specs + [vm]
    else:
        operands += tables + list(state)
        specs += [sm] * len(tables) + [vm, hb]
        aliases = {len(specs) - 1: 2}
    work = 26 * n // 2
    return pl.pallas_call(
        functools.partial(pair_kernel, steps, len(tables)),
        out_shape=outs,
        in_specs=specs,
        out_specs=out_specs,
        scratch_shapes=[
            pltpu.SMEM((8, n * 16 + 8), jnp.int32),
            pltpu.SMEM((n * 4, 128), jnp.int32),
            pltpu.VMEM((n * 4, 128), jnp.int32),
            pltpu.VMEM((n * 4, 32, 128), bf16),
            pltpu.VMEM((n * 4, META, 128), bf16),
            pltpu.VMEM((n * 16 + 8, 128), f32),
            pltpu.VMEM((n * 16, 128), f32),
            pltpu.VMEM((DBS, 256), f32),
            pltpu.VMEM((DBS, 256), f32),
            pltpu.VMEM((DBS, 256), bf16),
            pltpu.VMEM((DBS, 256), bf16),
            pltpu.VMEM((RING, 2, DBS, 256), bf16),
            pltpu.SemaphoreType.DMA((RING,)),
            pltpu.SemaphoreType.DMA((n,)),
            pltpu.SemaphoreType.DMA((n,)),
        ],
        input_output_aliases=aliases,
        compiler_params=pltpu.CompilerParams(vmem_limit_bytes=14 << 20),
        cost_estimate=pl.CostEstimate(
            flops=work * 4 * DBS * PBS * 128, transcendentals=work * DBS * PBS, bytes_accessed=work * DBS * PBS * 2
        ),
        name="pairs",
    )(*operands)


def share_kernel(ta, tb, tc, inv_ref, low_ref, out_ref, share_ref, buf, sem):
    share_ref[...] = jnp.zeros_like(share_ref)
    depth = buf.shape[0]
    na, nb, nc = [(t[3, 0] + 1) // 2 for t in (ta, tb, tc)]
    n = na + nb + nc

    def entry(k, p, e):
        ea = jnp.minimum(2 * p + e, TABLE - 1)
        eb = jnp.clip(2 * (p - na) + e, 0, TABLE - 1)
        ec = jnp.maximum(2 * (p - na - nb) + e, 0)
        return jnp.where(p < na, ta[k, ea], jnp.where(p < na + nb, tb[k, eb], tc[k, ec]))

    def copy_in(p, s):
        return pltpu.make_async_copy(low_ref.at[p], buf.at[s], sem.at[s])

    for d in range(depth):
        @pl.when(d < n)
        def _(d=d):
            copy_in(d, d).start()

    def one(p, s, e):
        a0, a1 = entry(0, p, e + 1) >> 8, entry(1, p, e + 1) >> 8
        r = jnp.minimum(entry(2, p, e + 1), 7)
        acc = jnp.zeros((8, 256), f32)
        for h in range(0, DBS, 64):
            v = inv_ref[r, h:h + 64, :]
            t = buf[s, e, h:h + 64, :].astype(f32) * jnp.concatenate([v, v], axis=1)
            acc = acc + jnp.sum(t.reshape(8, 8, 256), axis=0)
        return a0, a1, jnp.sum(acc, axis=0, keepdims=True)

    def step(p, carry):
        s = lax.rem(p, depth)
        copy_in(p, s).wait()
        done = [one(p, s, 0), one(p, s, 1)]
        for a0, a1, t in done:
            share_ref[pl.ds(a0, 1), :] += t[:, :128]
            share_ref[pl.ds(a1, 1), :] += t[:, 128:]

        @pl.when(p + depth < n)
        def _():
            copy_in(p + depth, s).start()

        return carry

    lax.fori_loop(0, n, step, 0)
    out_ref[...] = share_ref[0:NONE, :]


def share_call(tables, inv_b, low):
    vm = pl.BlockSpec(memory_space=pltpu.VMEM)
    sm = pl.BlockSpec(memory_space=pltpu.SMEM)
    hb = pl.BlockSpec(memory_space=pltpu.HBM)
    return pl.pallas_call(
        share_kernel,
        out_shape=jax.ShapeDtypeStruct((NONE, 128), f32),
        in_specs=[sm, sm, sm, vm, hb],
        out_specs=vm,
        scratch_shapes=[
            pltpu.VMEM((NONE + 8, 128), f32),
            pltpu.VMEM((RING, 2, DBS, 256), bf16),
            pltpu.SemaphoreType.DMA((RING,)),
        ],
        compiler_params=pltpu.CompilerParams(vmem_limit_bytes=30 << 20),
        cost_estimate=pl.CostEstimate(flops=104 * DBS * PBS * 2, transcendentals=0, bytes_accessed=104 * DBS * PBS * 2),
        name="shares",
    )(*tables, inv_b, low)


def local(particles, weights, detections, clutter, gate_ids, gate_lens):
    gx, gy = lax.axis_index("gx"), lax.axis_index("gy")
    c, alpha = gy % 2, gy // 2
    pos = jnp.stack([c, gy // 8, gy // 2 % 4]).astype(jnp.int32)

    half = jnp.sum(jnp.square(particles.astype(f32)), axis=1).reshape(8, PBS) * (-0.5 * SCALE)
    hi = lax.reduce_precision(half, 8, 7)
    mid = lax.reduce_precision(half - hi, 8, 7)
    lo = (half - hi) - mid
    live = jnp.arange(16, dtype=jnp.int32)[None, :] < gate_lens[:, None]
    bit = jnp.where(live, 1 << ((gate_ids // 32) * 2 + gate_ids % 2), 0)
    owner = (gate_ids % 32) // 2
    masks = jnp.sum(jnp.where(owner[:, None, :] == jnp.arange(16)[None, :, None], bit[:, None, :], 0), axis=2)
    rows = [weights.reshape(8, PBS), hi.astype(bf16), mid.astype(bf16), lo.astype(bf16)]
    sends = []
    for h in range(2):
        own = slice(h * HB, (h + 1) * HB)
        gate = jnp.transpose(masks[own]).reshape(1, 64).astype(bf16)
        sends.append(
            jnp.concatenate(
                [particles[h * META:(h + 1) * META]]
                + [v[own] for v in rows]
                + [jnp.pad(gate, ((0, 15), (0, 64)))]
            )
        )

    dets = lax.all_gather(jnp.stack([detections, gy_shift(detections, 0, 0, 1)]), "gx").reshape(8, DBS, 128)

    sends = lax.optimization_barrier(sends)
    first = [
        [sends[0]] + [gy_shift(sends[0], 0, s) for s in (1, 3, 2)],
        [sends[1]] + [gy_shift(sends[1], s, 0) for s in (1, 3, 2)],
    ]
    first = lax.optimization_barrier(first)
    halves = [jnp.stack([v[0], v[1], v[3], v[2]]) for v in first]

    second = [v for s in (1, 3) for v in (gy_shift(halves[0], s, 0), gy_shift(halves[1], 0, s))]
    mom1, mass1, low, ta, as_b = pair_call((0,), pos, halves, dets, [], None)
    sum1 = jnp.sum(mass1, axis=2)
    second, halves, sum1 = lax.optimization_barrier((second, halves, sum1))
    third = [gy_shift(halves[0], 2, 0), gy_shift(halves[1], 0, 2)]
    mom2, mass2, low, tb = pair_call((1, 3), pos, second, dets, [ta], (as_b, low))
    mom3, mass3, low, tc = pair_call((2,), pos, third, dets, [ta, tb], (as_b, low))

    part = (sum1 + jnp.sum(mass2 + mass3, axis=2))[:8].reshape(4, 2, DBS) * DETECT_PROB
    mine = (jnp.arange(4)[:, None, None] == gx) & (jnp.arange(2)[None, :, None] == 0)
    part = part + jnp.where(mine, clutter[None, None, :], 0.0)
    norm = part + gy_shift(part, 0, 0, 1)[:, ::-1]
    norm = norm + x_swap(norm, 1)
    norm = norm + x_swap(norm, 2)
    inv = (1.0 / norm).astype(bf16).astype(f32)
    inv_b = jnp.broadcast_to(inv.reshape(8, DBS)[:, :, None], (8, DBS, 128))

    far = mom1[4:8] + mom2[4:8] + mom3[4:8]
    own = mom1[0:4] + mom2[0:4] + mom3[0:4] + gy_shift(far, 0, 0, 1)
    inv_b, own = lax.optimization_barrier((inv_b, own))
    moment = lax.dynamic_index_in_dim(own, gx, 0, False)
    for s in (1, 2, 3):
        moment = moment + x_shift(lax.dynamic_index_in_dim(own, (gx + s) % 4, 0, False), s)
    normalizer = lax.dynamic_index_in_dim(norm[:, 0], gx, 0, False)

    share = share_call((ta, tb, tc), inv_b, low)
    share, moment = lax.optimization_barrier((share, moment))
    back = lax.all_to_all(
        share.reshape(16, 8, 128), "gy", split_axis=0, concat_axis=0, axis_index_groups=alpha_groups()
    )
    total = jnp.sum(back, axis=0).reshape(-1)
    updated = weights.astype(f32) * ((1.0 - DETECT_PROB) + DETECT_PROB * total)
    return updated, jnp.log(normalizer), DETECT_PROB * moment / normalizer[:, None]


def solution(mesh):
    both = P(("gx", "gy"))
    rows = P(("gx", "gy"), None)
    return jax.shard_map(
        local,
        mesh=mesh,
        in_specs=(rows, both, rows, both, rows, both),
        out_specs=(both, both, rows),
        check_vma=False,
    )
```

```python
import functools

import jax
import jax.numpy as jnp
from jax import lax
from jax.experimental import pallas as pl
from jax.experimental.pallas import tpu as pltpu
from jax.sharding import PartitionSpec as P

PBS = 128
DBS = 512
DETECT_PROB = 0.9
LOG2E = 1.4426950408889634
SCALE = LOG2E / 8.0
HB = 4
META = HB * PBS
ROWS = META + 32
TABLE = 152
LOW = 100
RING = 8
DUMMY = 8
NONE = 128

f32 = jnp.float32
bf16 = jnp.bfloat16


def alpha_groups():
    return [[a * 2 + c for a in range(16)] for c in range(2)]


def gy_shift(v, dz, dy, dc=0):
    perm = []
    for i in range(32):
        z, y, c = i // 8, i // 2 % 4, i % 2
        perm.append((i, (z + dz) % 4 * 8 + (y + dy) % 4 * 2 + (c + dc) % 2))
    return lax.ppermute(v, "gy", perm)


def x_shift(v, s):
    return lax.ppermute(v, "gx", [(i, (i + s) % 4) for i in range(4)])


def x_swap(v, s):
    return lax.ppermute(v, "gx", [(i, i ^ s) for i in range(4)])


def prep_kernel(ids_ref, lens_ref, part_ref, weight_ref, out0_ref, out1_ref, rows):
    ones = jnp.ones((8, 128), bf16)
    lanes = lax.broadcasted_iota(jnp.int32, (8, 128), 1)
    weights = weight_ref[...].astype(f32)
    for h, out_ref in enumerate((out0_ref, out1_ref)):
        out_ref[0:META, :] = part_ref[h * META:(h + 1) * META, :]
        gate = jnp.zeros((8, 128), jnp.int32)
        for j in range(HB):
            b = h * HB + j
            block = part_ref[b * PBS:(b + 1) * PBS, :].astype(f32)
            square = block * block
            hi = square.astype(bf16)
            lo = (square - hi.astype(f32)).astype(bf16)
            total = sum(
                lax.dot_general(ones, v, (((1,), (1,)), ((), ())), preferred_element_type=f32) for v in (hi, lo)
            )
            total = total[0:1] * (-0.5 * SCALE)
            rows[j:j + 1, :] = weights[b:b + 1]
            for k in range(1, 4):
                piece = total.astype(bf16).astype(f32)
                rows[k * HB + j:k * HB + j + 1, :] = piece
                total = total - piece
            for g in range(16):
                d = ids_ref[b, g]
                at = jnp.where(g < lens_ref[b], (d % 32) // 2 * HB + j, -1)
                gate = gate + jnp.where(lanes == at, 1 << (d // 32 * 2 + d % 2), 0)
        out_ref[META:META + 16, :] = rows[...].astype(bf16)
        gate = gate.astype(f32)
        out_ref[META + 16:META + 32, :] = jnp.concatenate([gate, gate], axis=0).astype(bf16)


def prep_call(particles, weights, gate_ids, gate_lens):
    vm = pl.BlockSpec(memory_space=pltpu.VMEM)
    sm = pl.BlockSpec(memory_space=pltpu.SMEM)
    half = jax.ShapeDtypeStruct((ROWS, 128), bf16)
    return pl.pallas_call(
        prep_kernel,
        out_shape=(half, half),
        in_specs=[sm, sm, vm, vm],
        out_specs=(vm, vm),
        scratch_shapes=[pltpu.VMEM((16, 128), f32)],
        name="payload",
    )(gate_ids, gate_lens, particles, weights.reshape(8, PBS))


def pair_kernel(steps, before, last, *refs):
    parts = 2 * len(steps)
    count = parts * 16
    pos_ref, refs = refs[0], refs[1:]
    part_refs, refs = refs[:parts], refs[parts:]
    det_ref, refs = refs[0], refs[1:]
    first = before == 0
    tables, refs = refs[:before], refs[before:]
    if not first:
        mom_in, mass_in, as_ref, refs = refs[0], refs[1], refs[2], refs[4:]
    if last:
        near_ref, far_ref = refs[:2]
        mom_ref, done = refs[-2:]
        refs = refs[2:-2]
    else:
        mom_ref, refs = refs[0], refs[1:]
    mass_ref, low_ref, slot_ref, refs = refs[0], refs[1], refs[2], refs[3:]
    if first:
        as_ref, refs = refs[0], refs[1:]
    lst, gates, grow, meta, xs, wrow, brow, cr0, cr1, w0, w1, ring, sem, xsem, msem = refs
    c, z, y = pos_ref[0], pos_ref[1], pos_ref[2]
    lane = (z * 4 + y) * HB

    heads = [
        pltpu.make_async_copy(part_refs[t].at[:, pl.ds(META, 32), :], meta.at[pl.ds(4 * t, 4)], msem.at[t])
        for t in range(parts)
    ]
    loads = [
        pltpu.make_async_copy(part_refs[t].at[:, pl.ds(0, META), :], xs.at[pl.ds(4 * t, 4)], xsem.at[t])
        for t in range(parts)
    ]
    for copy in heads + loads:
        copy.start()
    if first:
        mom_ref[...] = jnp.zeros_like(mom_ref)
        mass_ref[...] = jnp.zeros_like(mass_ref)
        for r in range(8):
            for h in range(0, DBS, 128):
                d = det_ref[r, h:h + 128, :].astype(f32)
                v = jnp.sum(d * d, axis=1, keepdims=True) * (-0.5 * SCALE) + 16.0 * LOG2E
                as_ref[r, h:h + 128, :] = jnp.broadcast_to(v, (128, 128))
    else:
        mom_ref[...] = mom_in[...]
        mass_ref[...] = mass_in[...]
    base = jnp.int32(0)
    for table in tables:
        base = base + (table[3, 0] + 1) // 2
    for copy in heads:
        copy.wait()
    for s in range(parts * 4):
        grow[s:s + 1, :] = meta[s, 16:32, :].astype(f32)[0:1].astype(jnp.int32)
    gate_load = pltpu.make_async_copy(grow, gates, msem.at[0])
    gate_load.start()
    for s in range(parts * 4):
        rows = meta[s, 0:16, :].astype(f32)
        wrow[s * 4:(s + 1) * 4, :] = rows[0:4]
        brow[s * 4:(s + 1) * 4, :] = rows[4:8] + rows[8:12] + rows[12:16]
    wrow[count:count + 8, :] = jnp.zeros((8, 128), f32)
    gate_load.wait()

    counts = [jnp.int32(0)] * 8
    for s in range(parts * 4):
        h, step, u = s // 4 % 2, steps[s // 8], s % 4
        dz, dy = (step, u) if h == 0 else (u, step)
        home = (((z + 4 - dz) % 4) * 4 + (y + 4 - dy) % 4) * 8 + h * 4
        for j in range(HB):
            m = gates[s, lane + j]
            v = (home + j) * 256 + (s * 4 + j)
            for r in range(8):
                lst[r, counts[r]] = v
                counts[r] = counts[r] + ((m >> r) & 1)

    def put(q, v0, v1, r):
        slot_ref[0, q] = v0
        slot_ref[1, q] = v1
        slot_ref[2, q] = r

    hole = NONE * 256 + count
    put(0, 0, hole, DUMMY)
    q = jnp.int32(1)
    for r in range(8):
        cnt = counts[r]

        def fill(p, q, r=r, cnt=cnt):
            put(q, lst[r, 2 * p], jnp.where(2 * p + 1 < cnt, lst[r, 2 * p + 1], hole), r)
            return q + 1

        q = lax.fori_loop(0, (cnt + 1) // 2, fill, q)
    for d in range(3):
        put(q + d, NONE * 256, hole, DUMMY)
    n = q - 1
    slot_ref[3, 0] = n
    for copy in loads:
        copy.wait()

    cr, w = (cr0, cr1), (w0, w1)

    def copy_out(p, j):
        return pltpu.make_async_copy(ring.at[j], low_ref.at[p], sem.at[j])

    def both(q):
        b0 = slot_ref[0, q] & 255
        b1 = jnp.minimum(slot_ref[1, q] & 255, count - 1)
        return jnp.concatenate(
            [xs[b // 4, pl.ds(pl.multiple_of(b % 4 * PBS, PBS), PBS), :] for b in (b0, b1)], axis=0
        )

    def cross(q, s):
        r = jnp.minimum(slot_ref[2, q], 7)
        cr[s][...] = lax.dot_general(det_ref[r], both(q), (((1,), (1,)), ((), ())), preferred_element_type=f32)

    def likelihood(q, s, j):
        b0, b1, r = slot_ref[0, q] & 255, slot_ref[1, q] & 255, slot_ref[2, q]
        b1c, rc = jnp.minimum(b1, count - 1), jnp.minimum(r, 7)
        w2 = jnp.concatenate([wrow[pl.ds(b0, 1), :], wrow[pl.ds(b1, 1), :]], axis=1)
        s2 = jnp.concatenate([brow[pl.ds(b0, 1), :], brow[pl.ds(b1c, 1), :]], axis=1)
        for h in range(0, DBS, 32):
            rows = slice(h, h + 32)
            a = as_ref[rc, rows, :]
            lik = jnp.exp2(cr[s][rows, :] * SCALE + (jnp.concatenate([a, a], axis=1) + s2))
            ring[j, 1 - s, rows, :] = lik.astype(bf16)
            wtd = lik * w2
            mass_ref[r, rows, :] += wtd[:, :128] + wtd[:, 128:]
            w[s][rows, :] = wtd.astype(bf16)

    def moment(q, s):
        mom_ref[slot_ref[2, q]] += jnp.dot(w[s][...], both(q), preferred_element_type=f32)

    cross(1, 1)

    def body(p, carry):
        q = 2 * p + 2
        j = lax.rem(p, RING)

        @pl.when(p >= RING)
        def _():
            copy_out(0, j).wait()

        cross(q, 0)
        likelihood(q - 1, 1, j)
        moment(q - 2, 0)
        cross(q + 1, 1)
        likelihood(q, 0, j)
        moment(q - 1, 1)
        copy_out(base + p, j).start()
        return carry

    total = (n + 2) // 2
    lax.fori_loop(0, total, body, 0)

    def drain(j, carry):
        copy_out(0, j).wait()
        return carry

    if last:
        out = [
            pltpu.make_async_copy(mom_ref.at[2 * k + (c ^ d)], (near_ref, far_ref)[d].at[k], done.at[2 * k + d])
            for d in (1, 0)
            for k in range(4)
        ]
        for copy in out:
            copy.start()
    lax.fori_loop(0, jnp.minimum(total, RING), drain, 0)
    if last:
        for copy in out:
            copy.wait()


def pair_call(steps, last, pos, parts, dets, tables, state):
    n = len(parts)
    first = state is None
    vm = pl.BlockSpec(memory_space=pltpu.VMEM)
    sm = pl.BlockSpec(memory_space=pltpu.SMEM)
    hb = pl.BlockSpec(memory_space=pl.ANY)
    acc = jax.ShapeDtypeStruct((9, DBS, 128), f32)
    half = jax.ShapeDtypeStruct((4, DBS, 128), f32)
    low = jax.ShapeDtypeStruct((LOW, 2, DBS, 256), bf16)
    table = jax.ShapeDtypeStruct((4, TABLE), jnp.int32)
    operands, specs = [pos] + parts + [dets], [sm] + [hb] * n + [vm]
    outs, out_specs = [acc, acc, low, table], [vm, vm, hb, sm]
    aliases, extra = {}, []
    if first:
        outs, out_specs = outs + [jax.ShapeDtypeStruct((8, DBS, 128), f32)], out_specs + [vm]
    else:
        operands += tables + list(state)
        specs += [sm] * len(tables) + [vm, vm, vm, hb]
        aliases = {len(specs) - 1: 2 + last}
    if last:
        outs, out_specs = [half, half] + outs[1:], [hb, hb] + out_specs[1:]
        extra = [pltpu.VMEM((9, DBS, 128), f32), pltpu.SemaphoreType.DMA((8,))]
    work = 26 * n // 2
    return pl.pallas_call(
        functools.partial(pair_kernel, steps, len(tables), last),
        out_shape=outs,
        in_specs=specs,
        out_specs=out_specs,
        scratch_shapes=[
            pltpu.SMEM((8, n * 16 + 8), jnp.int32),
            pltpu.SMEM((n * 4, 128), jnp.int32),
            pltpu.VMEM((n * 4, 128), jnp.int32),
            pltpu.VMEM((n * 4, 32, 128), bf16),
            pltpu.VMEM((n * 4, META, 128), bf16),
            pltpu.VMEM((n * 16 + 8, 128), f32),
            pltpu.VMEM((n * 16, 128), f32),
            pltpu.VMEM((DBS, 256), f32),
            pltpu.VMEM((DBS, 256), f32),
            pltpu.VMEM((DBS, 256), bf16),
            pltpu.VMEM((DBS, 256), bf16),
            pltpu.VMEM((RING, 2, DBS, 256), bf16),
            pltpu.SemaphoreType.DMA((RING,)),
            pltpu.SemaphoreType.DMA((n,)),
            pltpu.SemaphoreType.DMA((n,)),
        ] + extra,
        input_output_aliases=aliases,
        compiler_params=pltpu.CompilerParams(vmem_limit_bytes=14 << 20),
        cost_estimate=pl.CostEstimate(
            flops=work * 4 * DBS * PBS * 128, transcendentals=work * DBS * PBS, bytes_accessed=work * DBS * PBS * 2
        ),
        name="pairs",
    )(*operands)


def share_kernel(ta, tb, tc, inv_ref, low_ref, out_ref, share_ref, buf, sem):
    share_ref[...] = jnp.zeros_like(share_ref)
    depth = buf.shape[0]
    na, nb, nc = [(t[3, 0] + 1) // 2 for t in (ta, tb, tc)]
    n = na + nb + nc

    def entry(k, p, e):
        ea = jnp.minimum(2 * p + e, TABLE - 1)
        eb = jnp.clip(2 * (p - na) + e, 0, TABLE - 1)
        ec = jnp.maximum(2 * (p - na - nb) + e, 0)
        return jnp.where(p < na, ta[k, ea], jnp.where(p < na + nb, tb[k, eb], tc[k, ec]))

    def copy_in(p, s):
        return pltpu.make_async_copy(low_ref.at[p], buf.at[s], sem.at[s])

    for d in range(depth):
        @pl.when(d < n)
        def _(d=d):
            copy_in(d, d).start()

    def one(p, s, e):
        a0, a1 = entry(0, p, e + 1) >> 8, entry(1, p, e + 1) >> 8
        r = jnp.minimum(entry(2, p, e + 1), 7)
        acc = jnp.zeros((8, 256), f32)
        for h in range(0, DBS, 64):
            v = inv_ref[r, h:h + 64, :]
            t = buf[s, e, h:h + 64, :].astype(f32) * jnp.concatenate([v, v], axis=1)
            acc = acc + jnp.sum(t.reshape(8, 8, 256), axis=0)
        return a0, a1, jnp.sum(acc, axis=0, keepdims=True)

    def step(p, carry):
        s = lax.rem(p, depth)
        copy_in(p, s).wait()
        done = [one(p, s, 0), one(p, s, 1)]
        for a0, a1, t in done:
            share_ref[pl.ds(a0, 1), :] += t[:, :128]
            share_ref[pl.ds(a1, 1), :] += t[:, 128:]

        @pl.when(p + depth < n)
        def _():
            copy_in(p + depth, s).start()

        return carry

    lax.fori_loop(0, n, step, 0)
    out_ref[...] = share_ref[0:NONE, :]


def share_call(tables, inv_b, low):
    vm = pl.BlockSpec(memory_space=pltpu.VMEM)
    sm = pl.BlockSpec(memory_space=pltpu.SMEM)
    hb = pl.BlockSpec(memory_space=pltpu.HBM)
    return pl.pallas_call(
        share_kernel,
        out_shape=jax.ShapeDtypeStruct((NONE, 128), f32),
        in_specs=[sm, sm, sm, vm, hb],
        out_specs=vm,
        scratch_shapes=[
            pltpu.VMEM((NONE + 8, 128), f32),
            pltpu.VMEM((RING, 2, DBS, 256), bf16),
            pltpu.SemaphoreType.DMA((RING,)),
        ],
        compiler_params=pltpu.CompilerParams(vmem_limit_bytes=14 << 20),
        cost_estimate=pl.CostEstimate(flops=104 * DBS * PBS * 2, transcendentals=0, bytes_accessed=104 * DBS * PBS * 2),
        name="shares",
    )(*tables, inv_b, low)


def local(particles, weights, detections, clutter, gate_ids, gate_lens):
    gx, gy = lax.axis_index("gx"), lax.axis_index("gy")
    c, alpha = gy % 2, gy // 2
    pos = jnp.stack([c, gy // 8, gy // 2 % 4]).astype(jnp.int32)

    groups = [[x * 32 + a * 2 + d for x in range(4) for d in range(2)] for a in range(16)]
    dets = lax.all_gather(detections, ("gx", "gy"), axis_index_groups=groups)

    sends = prep_call(particles, weights, gate_ids, gate_lens)
    first = [
        [sends[0]] + [gy_shift(sends[0], 0, s) for s in (1, 3, 2)],
        [sends[1]] + [gy_shift(sends[1], s, 0) for s in (1, 3, 2)],
    ]
    first = lax.optimization_barrier(first)
    halves = [jnp.stack([v[0], v[1], v[3], v[2]]) for v in first]

    second = [v for s in (1, 3) for v in (gy_shift(halves[0], s, 0), gy_shift(halves[1], 0, s))]
    mom, mass, low, ta, as_b = pair_call((0,), False, pos, halves, dets, [], None)
    second, halves, ta = lax.optimization_barrier((second, halves, ta))
    third = [gy_shift(halves[0], 2, 0), gy_shift(halves[1], 0, 2)]
    mom, mass, low, tb = pair_call((1, 3), False, pos, second, dets, [ta], (mom, mass, as_b, low))
    near, far, mass, low, tc = pair_call((2,), True, pos, third, dets, [ta, tb], (mom, mass, as_b, low))

    part = jnp.sum(mass, axis=2)[:8].reshape(4, 2, DBS) * DETECT_PROB
    mine = (jnp.arange(4)[:, None, None] == gx) & (jnp.arange(2)[None, :, None] == c)
    part = part + jnp.where(mine, clutter[None, None, :], 0.0)
    norm = part + gy_shift(part, 0, 0, 1)
    norm = norm + x_swap(norm, 1)
    own = near + gy_shift(far, 0, 0, 1)
    norm, own = lax.optimization_barrier((norm, own))
    norm = norm + x_swap(norm, 2)
    inv = (1.0 / norm).astype(bf16).astype(f32)
    inv_b = jnp.broadcast_to(inv.reshape(8, DBS)[:, :, None], (8, DBS, 128))

    moment = lax.dynamic_index_in_dim(own, gx, 0, False)
    for s in (1, 2, 3):
        moment = moment + x_shift(lax.dynamic_index_in_dim(own, (gx + s) % 4, 0, False), s)
    normalizer = lax.dynamic_index_in_dim(norm.reshape(8, DBS), gx * 2 + c, 0, False)

    share = share_call((ta, tb, tc), inv_b, low)
    share, moment = lax.optimization_barrier((share, moment))
    back = lax.all_to_all(
        share.reshape(16, 8, 128), "gy", split_axis=0, concat_axis=0, axis_index_groups=alpha_groups()
    )
    total = jnp.sum(back, axis=0).reshape(-1)
    updated = weights.astype(f32) * ((1.0 - DETECT_PROB) + DETECT_PROB * total)
    return updated, jnp.log(normalizer), DETECT_PROB * moment / normalizer[:, None]


def solution(mesh):
    both = P(("gx", "gy"))
    rows = P(("gx", "gy"), None)
    return jax.shard_map(
        local,
        mesh=mesh,
        in_specs=(rows, both, rows, both, rows, both),
        out_specs=(both, both, rows),
        check_vma=False,
    )
```

```python
import functools

import jax
import jax.numpy as jnp
from jax import lax
from jax.experimental import pallas as pl
from jax.experimental.pallas import tpu as pltpu
from jax.sharding import PartitionSpec as P

PBS = 128
DBS = 512
DETECT_PROB = 0.9
LOG2E = 1.4426950408889634
SCALE = LOG2E / 8.0
HB = 4
META = HB * PBS
ROWS = META + 32
TABLE = 152
LOW = 100
RING = 8
DUMMY = 8
NONE = 128

f32 = jnp.float32
bf16 = jnp.bfloat16


def alpha_groups():
    return [[a * 2 + c for a in range(16)] for c in range(2)]


def gy_shift(v, dz, dy, dc=0):
    perm = []
    for i in range(32):
        z, y, c = i // 8, i // 2 % 4, i % 2
        perm.append((i, (z + dz) % 4 * 8 + (y + dy) % 4 * 2 + (c + dc) % 2))
    return lax.ppermute(v, "gy", perm)


def x_shift(v, s):
    return lax.ppermute(v, "gx", [(i, (i + s) % 4) for i in range(4)])


def x_swap(v, s):
    return lax.ppermute(v, "gx", [(i, i ^ s) for i in range(4)])


def prep_kernel(ids_ref, lens_ref, part_ref, weight_ref, out0_ref, out1_ref, rows):
    ones = jnp.ones((8, 128), bf16)
    lanes = lax.broadcasted_iota(jnp.int32, (8, 128), 1)
    weights = weight_ref[...].astype(f32)
    for h, out_ref in enumerate((out0_ref, out1_ref)):
        out_ref[0:META, :] = part_ref[h * META:(h + 1) * META, :]
        gate = jnp.zeros((8, 128), jnp.int32)
        for j in range(HB):
            b = h * HB + j
            block = part_ref[b * PBS:(b + 1) * PBS, :].astype(f32)
            square = block * block
            hi = square.astype(bf16)
            lo = (square - hi.astype(f32)).astype(bf16)
            total = sum(
                lax.dot_general(ones, v, (((1,), (1,)), ((), ())), preferred_element_type=f32) for v in (hi, lo)
            )
            total = total[0:1] * (-0.5 * SCALE)
            rows[j:j + 1, :] = weights[b:b + 1]
            for k in range(1, 4):
                piece = total.astype(bf16).astype(f32)
                rows[k * HB + j:k * HB + j + 1, :] = piece
                total = total - piece
            for g in range(16):
                d = ids_ref[b, g]
                at = jnp.where(g < lens_ref[b], (d % 32) // 2 * HB + j, -1)
                gate = gate + jnp.where(lanes == at, 1 << (d // 32 * 2 + d % 2), 0)
        out_ref[META:META + 16, :] = rows[...].astype(bf16)
        gate = gate.astype(f32)
        out_ref[META + 16:META + 32, :] = jnp.concatenate([gate, gate], axis=0).astype(bf16)


def prep_call(particles, weights, gate_ids, gate_lens):
    vm = pl.BlockSpec(memory_space=pltpu.VMEM)
    sm = pl.BlockSpec(memory_space=pltpu.SMEM)
    half = jax.ShapeDtypeStruct((ROWS, 128), bf16)
    return pl.pallas_call(
        prep_kernel,
        out_shape=(half, half),
        in_specs=[sm, sm, vm, vm],
        out_specs=(vm, vm),
        scratch_shapes=[pltpu.VMEM((16, 128), f32)],
        name="payload",
    )(gate_ids, gate_lens, particles, weights.reshape(8, PBS))


def pair_kernel(steps, before, last, *refs):
    parts = 2 * len(steps)
    count = parts * 16
    pos_ref, refs = refs[0], refs[1:]
    part_refs, refs = refs[:parts], refs[parts:]
    det_ref, refs = refs[0], refs[1:]
    first = before == 0
    tables, refs = refs[:before], refs[before:]
    if not first:
        mom_in, mass_in, as_ref, refs = refs[0], refs[1], refs[2], refs[4:]
    if last:
        near_ref, far_ref = refs[:2]
        mom_ref, done = refs[-2:]
        refs = refs[2:-2]
    else:
        mom_ref, refs = refs[0], refs[1:]
    mass_ref, low_ref, slot_ref, refs = refs[0], refs[1], refs[2], refs[3:]
    if first:
        as_ref, refs = refs[0], refs[1:]
    lst, gates, grow, meta, xs, wrow, brow, cr0, cr1, w0, w1, ring, sem, xsem, msem = refs
    c, z, y = pos_ref[0], pos_ref[1], pos_ref[2]
    lane = (z * 4 + y) * HB

    heads = [
        pltpu.make_async_copy(part_refs[t].at[:, pl.ds(META, 32), :], meta.at[pl.ds(4 * t, 4)], msem.at[t])
        for t in range(parts)
    ]
    loads = [
        pltpu.make_async_copy(part_refs[t].at[:, pl.ds(0, META), :], xs.at[pl.ds(4 * t, 4)], xsem.at[t])
        for t in range(parts)
    ]
    for copy in heads + loads:
        copy.start()
    if first:
        mom_ref[...] = jnp.zeros_like(mom_ref)
        mass_ref[...] = jnp.zeros_like(mass_ref)
        for r in range(8):
            for h in range(0, DBS, 128):
                d = det_ref[r, h:h + 128, :].astype(f32)
                v = jnp.sum(d * d, axis=1, keepdims=True) * (-0.5 * SCALE) + 16.0 * LOG2E
                as_ref[r, h:h + 128, :] = jnp.broadcast_to(v, (128, 128))
    elif last:
        mom_ref[...] = mom_in[...]
        mass_ref[...] = mass_in[...]
    base = jnp.int32(0)
    for table in tables:
        base = base + (table[3, 0] + 1) // 2
    for copy in heads:
        copy.wait()
    for s in range(parts * 4):
        grow[s:s + 1, :] = meta[s, 16:32, :].astype(f32)[0:1].astype(jnp.int32)
    gate_load = pltpu.make_async_copy(grow, gates, msem.at[0])
    gate_load.start()
    for s in range(parts * 4):
        rows = meta[s, 0:16, :].astype(f32)
        wrow[s * 4:(s + 1) * 4, :] = rows[0:4]
        brow[s * 4:(s + 1) * 4, :] = rows[4:8] + rows[8:12] + rows[12:16]
    wrow[count:count + 8, :] = jnp.zeros((8, 128), f32)
    gate_load.wait()

    counts = [jnp.int32(0)] * 8
    for s in range(parts * 4):
        h, step, u = s // 4 % 2, steps[s // 8], s % 4
        dz, dy = (step, u) if h == 0 else (u, step)
        home = (((z + 4 - dz) % 4) * 4 + (y + 4 - dy) % 4) * 8 + h * 4
        for j in range(HB):
            m = gates[s, lane + j]
            v = (home + j) * 256 + (s * 4 + j)
            for r in range(8):
                lst[r, counts[r]] = v
                counts[r] = counts[r] + ((m >> r) & 1)

    def put(q, v0, v1, r):
        slot_ref[0, q] = v0
        slot_ref[1, q] = v1
        slot_ref[2, q] = r

    hole = NONE * 256 + count
    put(0, 0, hole, DUMMY)
    q = jnp.int32(1)
    for r in range(8):
        cnt = counts[r]

        def fill(p, q, r=r, cnt=cnt):
            put(q, lst[r, 2 * p], jnp.where(2 * p + 1 < cnt, lst[r, 2 * p + 1], hole), r)
            return q + 1

        q = lax.fori_loop(0, (cnt + 1) // 2, fill, q)
    for d in range(3):
        put(q + d, NONE * 256, hole, DUMMY)
    n = q - 1
    slot_ref[3, 0] = n
    for copy in loads:
        copy.wait()

    cr, w = (cr0, cr1), (w0, w1)

    def copy_out(p, j):
        return pltpu.make_async_copy(ring.at[j], low_ref.at[p], sem.at[j])

    def both(q):
        b0 = slot_ref[0, q] & 255
        b1 = jnp.minimum(slot_ref[1, q] & 255, count - 1)
        return jnp.concatenate(
            [xs[b // 4, pl.ds(pl.multiple_of(b % 4 * PBS, PBS), PBS), :] for b in (b0, b1)], axis=0
        )

    def cross(q, s):
        r = jnp.minimum(slot_ref[2, q], 7)
        cr[s][...] = lax.dot_general(det_ref[r], both(q), (((1,), (1,)), ((), ())), preferred_element_type=f32)

    def likelihood(q, s, j):
        b0, b1, r = slot_ref[0, q] & 255, slot_ref[1, q] & 255, slot_ref[2, q]
        b1c, rc = jnp.minimum(b1, count - 1), jnp.minimum(r, 7)
        w2 = jnp.concatenate([wrow[pl.ds(b0, 1), :], wrow[pl.ds(b1, 1), :]], axis=1)
        s2 = jnp.concatenate([brow[pl.ds(b0, 1), :], brow[pl.ds(b1c, 1), :]], axis=1)
        for h in range(0, DBS, 32):
            rows = slice(h, h + 32)
            a = as_ref[rc, rows, :]
            lik = jnp.exp2(cr[s][rows, :] * SCALE + (jnp.concatenate([a, a], axis=1) + s2))
            ring[j, 1 - s, rows, :] = lik.astype(bf16)
            wtd = lik * w2
            mass_ref[r, rows, :] += wtd[:, :128] + wtd[:, 128:]
            w[s][rows, :] = wtd.astype(bf16)

    def moment(q, s):
        mom_ref[slot_ref[2, q]] += jnp.dot(w[s][...], both(q), preferred_element_type=f32)

    cross(1, 1)

    def body(p, carry):
        q = 2 * p + 2
        j = lax.rem(p, RING)

        @pl.when(p >= RING)
        def _():
            copy_out(0, j).wait()

        cross(q, 0)
        likelihood(q - 1, 1, j)
        moment(q - 2, 0)
        cross(q + 1, 1)
        likelihood(q, 0, j)
        moment(q - 1, 1)
        copy_out(base + p, j).start()
        return carry

    total = (n + 2) // 2
    lax.fori_loop(0, total, body, 0)

    def drain(j, carry):
        copy_out(0, j).wait()
        return carry

    if last:
        out = [
            pltpu.make_async_copy(mom_ref.at[2 * k + (c ^ d)], (near_ref, far_ref)[d].at[k], done.at[2 * k + d])
            for d in (1, 0)
            for k in range(4)
        ]
        for copy in out:
            copy.start()
    lax.fori_loop(0, jnp.minimum(total, RING), drain, 0)
    if last:
        for copy in out:
            copy.wait()


def pair_call(steps, last, pos, parts, dets, tables, state):
    n = len(parts)
    first = state is None
    vm = pl.BlockSpec(memory_space=pltpu.VMEM)
    sm = pl.BlockSpec(memory_space=pltpu.SMEM)
    hb = pl.BlockSpec(memory_space=pl.ANY)
    acc = jax.ShapeDtypeStruct((9, DBS, 128), f32)
    half = jax.ShapeDtypeStruct((4, DBS, 128), f32)
    low = jax.ShapeDtypeStruct((LOW, 2, DBS, 256), bf16)
    table = jax.ShapeDtypeStruct((4, TABLE), jnp.int32)
    operands, specs = [pos] + parts + [dets], [sm] + [hb] * n + [vm]
    outs, out_specs = [acc, acc, low, table], [vm, vm, hb, sm]
    aliases, extra = {}, []
    if first:
        outs, out_specs = outs + [jax.ShapeDtypeStruct((8, DBS, 128), f32)], out_specs + [vm]
    else:
        operands += tables + list(state)
        specs += [sm] * len(tables) + [vm, vm, vm, hb]
        aliases = {len(specs) - 1: 2 + last}
        if not last:
            aliases.update({len(specs) - 4: 0, len(specs) - 3: 1})
    if last:
        outs, out_specs = [half, half] + outs[1:], [hb, hb] + out_specs[1:]
        extra = [pltpu.VMEM((9, DBS, 128), f32), pltpu.SemaphoreType.DMA((8,))]
    work = 26 * n // 2
    return pl.pallas_call(
        functools.partial(pair_kernel, steps, len(tables), last),
        out_shape=outs,
        in_specs=specs,
        out_specs=out_specs,
        scratch_shapes=[
            pltpu.SMEM((8, n * 16 + 8), jnp.int32),
            pltpu.SMEM((n * 4, 128), jnp.int32),
            pltpu.VMEM((n * 4, 128), jnp.int32),
            pltpu.VMEM((n * 4, 32, 128), bf16),
            pltpu.VMEM((n * 4, META, 128), bf16),
            pltpu.VMEM((n * 16 + 8, 128), f32),
            pltpu.VMEM((n * 16, 128), f32),
            pltpu.VMEM((DBS, 256), f32),
            pltpu.VMEM((DBS, 256), f32),
            pltpu.VMEM((DBS, 256), bf16),
            pltpu.VMEM((DBS, 256), bf16),
            pltpu.VMEM((RING, 2, DBS, 256), bf16),
            pltpu.SemaphoreType.DMA((RING,)),
            pltpu.SemaphoreType.DMA((n,)),
            pltpu.SemaphoreType.DMA((n,)),
        ] + extra,
        input_output_aliases=aliases,
        compiler_params=pltpu.CompilerParams(vmem_limit_bytes=14 << 20),
        cost_estimate=pl.CostEstimate(
            flops=work * 4 * DBS * PBS * 128, transcendentals=work * DBS * PBS, bytes_accessed=work * DBS * PBS * 2
        ),
        name="pairs",
    )(*operands)


def share_kernel(ta, tb, tc, inv_ref, low_ref, out_ref, share_ref, buf, sem):
    share_ref[...] = jnp.zeros_like(share_ref)
    depth = buf.shape[0]
    na, nb, nc = [(t[3, 0] + 1) // 2 for t in (ta, tb, tc)]
    n = na + nb + nc

    def entry(k, p, e):
        ea = jnp.minimum(2 * p + e, TABLE - 1)
        eb = jnp.clip(2 * (p - na) + e, 0, TABLE - 1)
        ec = jnp.maximum(2 * (p - na - nb) + e, 0)
        return jnp.where(p < na, ta[k, ea], jnp.where(p < na + nb, tb[k, eb], tc[k, ec]))

    def copy_in(p, s):
        return pltpu.make_async_copy(low_ref.at[p], buf.at[s], sem.at[s])

    for d in range(depth):
        @pl.when(d < n)
        def _(d=d):
            copy_in(d, d).start()

    def one(p, s, e):
        a0, a1 = entry(0, p, e + 1) >> 8, entry(1, p, e + 1) >> 8
        r = jnp.minimum(entry(2, p, e + 1), 7)
        acc = jnp.zeros((8, 256), f32)
        for h in range(0, DBS, 64):
            v = inv_ref[r, h:h + 64, :]
            t = buf[s, e, h:h + 64, :].astype(f32) * jnp.concatenate([v, v], axis=1)
            acc = acc + jnp.sum(t.reshape(8, 8, 256), axis=0)
        return a0, a1, jnp.sum(acc, axis=0, keepdims=True)

    def step(p, carry):
        s = lax.rem(p, depth)
        copy_in(p, s).wait()
        done = [one(p, s, 0), one(p, s, 1)]
        for a0, a1, t in done:
            share_ref[pl.ds(a0, 1), :] += t[:, :128]
            share_ref[pl.ds(a1, 1), :] += t[:, 128:]

        @pl.when(p + depth < n)
        def _():
            copy_in(p + depth, s).start()

        return carry

    lax.fori_loop(0, n, step, 0)
    out_ref[...] = share_ref[0:NONE, :]


def share_call(tables, inv_b, low):
    vm = pl.BlockSpec(memory_space=pltpu.VMEM)
    sm = pl.BlockSpec(memory_space=pltpu.SMEM)
    hb = pl.BlockSpec(memory_space=pltpu.HBM)
    return pl.pallas_call(
        share_kernel,
        out_shape=jax.ShapeDtypeStruct((NONE, 128), f32),
        in_specs=[sm, sm, sm, vm, hb],
        out_specs=vm,
        scratch_shapes=[
            pltpu.VMEM((NONE + 8, 128), f32),
            pltpu.VMEM((RING, 2, DBS, 256), bf16),
            pltpu.SemaphoreType.DMA((RING,)),
        ],
        compiler_params=pltpu.CompilerParams(vmem_limit_bytes=14 << 20),
        cost_estimate=pl.CostEstimate(flops=104 * DBS * PBS * 2, transcendentals=0, bytes_accessed=104 * DBS * PBS * 2),
        name="shares",
    )(*tables, inv_b, low)


def local(particles, weights, detections, clutter, gate_ids, gate_lens):
    gx, gy = lax.axis_index("gx"), lax.axis_index("gy")
    c, alpha = gy % 2, gy // 2
    pos = jnp.stack([c, gy // 8, gy // 2 % 4]).astype(jnp.int32)

    groups = [[x * 32 + a * 2 + d for x in range(4) for d in range(2)] for a in range(16)]
    dets = lax.all_gather(detections, ("gx", "gy"), axis_index_groups=groups)

    sends = prep_call(particles, weights, gate_ids, gate_lens)
    first = [
        [sends[0]] + [gy_shift(sends[0], 0, s) for s in (1, 3, 2)],
        [sends[1]] + [gy_shift(sends[1], s, 0) for s in (1, 3, 2)],
    ]
    first = lax.optimization_barrier(first)
    halves = [jnp.stack([v[0], v[1], v[3], v[2]]) for v in first]

    second = [v for s in (1, 3) for v in (gy_shift(halves[0], s, 0), gy_shift(halves[1], 0, s))]
    mom, mass, low, ta, as_b = pair_call((0,), False, pos, halves, dets, [], None)
    second, halves, ta = lax.optimization_barrier((second, halves, ta))
    third = [gy_shift(halves[0], 2, 0), gy_shift(halves[1], 0, 2)]
    mom, mass, low, tb = pair_call((1, 3), False, pos, second, dets, [ta], (mom, mass, as_b, low))
    near, far, mass, low, tc = pair_call((2,), True, pos, third, dets, [ta, tb], (mom, mass, as_b, low))

    part = jnp.sum(mass, axis=2)[:8].reshape(4, 2, DBS) * DETECT_PROB
    mine = (jnp.arange(4)[:, None, None] == gx) & (jnp.arange(2)[None, :, None] == c)
    part = part + jnp.where(mine, clutter[None, None, :], 0.0)
    norm = part + gy_shift(part, 0, 0, 1)
    norm = norm + x_swap(norm, 1)
    own = near + gy_shift(far, 0, 0, 1)
    norm, own = lax.optimization_barrier((norm, own))
    norm = norm + x_swap(norm, 2)
    inv = (1.0 / norm).astype(bf16).astype(f32)
    inv_b = jnp.broadcast_to(inv.reshape(8, DBS)[:, :, None], (8, DBS, 128))

    moment = lax.dynamic_index_in_dim(own, gx, 0, False)
    for s in (1, 2, 3):
        moment = moment + x_shift(lax.dynamic_index_in_dim(own, (gx + s) % 4, 0, False), s)
    normalizer = lax.dynamic_index_in_dim(norm.reshape(8, DBS), gx * 2 + c, 0, False)

    share = share_call((ta, tb, tc), inv_b, low)
    share, moment = lax.optimization_barrier((share, moment))
    back = lax.all_to_all(
        share.reshape(16, 8, 128), "gy", split_axis=0, concat_axis=0, axis_index_groups=alpha_groups()
    )
    total = jnp.sum(back, axis=0).reshape(-1)
    updated = weights.astype(f32) * ((1.0 - DETECT_PROB) + DETECT_PROB * total)
    return updated, jnp.log(normalizer), DETECT_PROB * moment / normalizer[:, None]


def solution(mesh):
    both = P(("gx", "gy"))
    rows = P(("gx", "gy"), None)
    return jax.shard_map(
        local,
        mesh=mesh,
        in_specs=(rows, both, rows, both, rows, both),
        out_specs=(both, both, rows),
        check_vma=False,
    )
```
